32 devices in a mesh: ctx: 8 (over z, x), tp: 4 (over y, core).
Axes of the slice: x: 2, y: 2, z: 4, core: 2. Of those that a mesh axis runs over, the one named last changes fastest.
Arguments:
- lin_q: bfloat16 [2048, 4096], P('ctx', 'tp'), may hold values from -6 to 6
- lin_k: bfloat16 [2048, 4096], P('ctx', 'tp'), may hold values from -6 to 6
- lin_v: bfloat16 [2048, 4096], P('ctx', 'tp'), may hold values from -20 to 20
- att_q: bfloat16 [2048, 4096], P('ctx', 'tp'), may hold values from -150 to 150
- att_k: bfloat16 [2048, 1024], P('ctx', 'tp'), may hold values from -7 to 7
- att_v: bfloat16 [2048, 1024], P('ctx', 'tp'), may hold values from -20 to 20
- block_lists: int32 [16, 4], P('ctx'), may hold values from -1 to 15, as said below
- gain_lin: bfloat16 [4096], P('tp'), may hold values from 0.25 to 1.75
- gain_att: bfloat16 [4096], P('tp'), may hold values from 0.25 to 1.75
Outputs:
- mixed: bfloat16 [2048, 4096], P('ctx', 'tp')
The draws below stay inside these ranges and needn't reach their ends.
Inputs may be any that keep to these rules, and one draw needn't show every extreme that they name: `block_lists`: row b: entry 0 is b; every other entry is either -1 (unused) or a block in b - 4 to b - 1, with no block twice; some row has all 4 entries in use.
All inputs are finite; a program needn't handle non-finite values.
Results may differ from the reference program's by a relative error of at most 0.0049.
Values may be sent and summed in bfloat16 or wider, within the bound.
A program may use at most 192 MiB of HBM per device.

```python
import jax
import jax.numpy as jnp
from jax import lax

HEADS = 32
KV_HEADS = 8
HD = 128
BLK = 128
SPAN = 5
LIST = 4
SEQ = 2048
NBLK = 16


def attention_pair(key):
    split_keys = jax.random.split(jax.random.fold_in(key, 7), 2)
    keys_all = jnp.clip(jax.random.normal(split_keys[1], (SEQ, KV_HEADS, HD), jnp.float32), -6.0, 6.0)
    queries = jnp.clip(jax.random.normal(split_keys[0], (SEQ, HEADS, HD), jnp.float32), -6.0, 6.0)
    return (queries.reshape(SEQ, HEADS * HD), keys_all.reshape(SEQ, KV_HEADS * HD))


def rising_values(key, heads):
    split_keys = jax.random.split(jax.random.fold_in(key, 3), 1)
    values = jnp.clip(jax.random.normal(split_keys[0], (SEQ, heads, HD), jnp.float32), -6.0, 6.0)
    rising = 3.0 ** (jnp.arange(heads, dtype=jnp.float32) / (heads - 1))
    return (values * rising[None, :, None]).reshape(SEQ, heads * HD).astype(jnp.bfloat16)


def draw_att_q(key, part):
    return attention_pair(key)[0].astype(jnp.bfloat16)


def draw_att_k(key, part):
    return attention_pair(key)[1].astype(jnp.bfloat16)


def draw_lin_v(key, part):
    return rising_values(jax.random.fold_in(key, 21), HEADS)


def draw_att_v(key, part):
    return rising_values(jax.random.fold_in(key, 22), KV_HEADS)


def draw_block_lists(key, part):
    split_keys = jax.random.split(jax.random.fold_in(key, 5), 2)
    block = jnp.arange(NBLK, dtype=jnp.int32)[:, None]
    offsets = jnp.arange(1, SPAN, dtype=jnp.int32)[None, :]
    random_part = jax.random.randint(split_keys[0], (NBLK, SPAN - 1), 0, 65536, jnp.int32)
    ranking = random_part * SPAN + offsets
    valid = block - offsets >= 0
    ranking = jnp.where(valid, ranking, -1 - offsets)
    chosen_rank, chosen_index = jax.lax.top_k(ranking, LIST - 1)
    chosen = block - (chosen_index.astype(jnp.int32) + 1)
    counts = jax.random.randint(split_keys[1], (NBLK, 1), 1, LIST + 1, jnp.int32)
    counts = jnp.where(block == NBLK - 1, LIST, counts)
    slots = jnp.arange(1, LIST, dtype=jnp.int32)[None, :]
    in_use = (slots < counts) & (chosen >= 0)
    others = jnp.where(in_use, chosen, -1)
    return jnp.concatenate([block, others], axis=1).astype(jnp.int32)


def steps_of(stream_key, dims, shards, smallest, top_value):
    gain, own = 1.0, jax.random.fold_in(stream_key, 6)
    for dim, shards_of in shards:
        heights = jnp.exp(jax.random.uniform(jax.random.fold_in(own, dim), (shards_of,), jnp.float32, smallest / len(shards), top_value / len(shards)))
        gain = gain * jnp.repeat(heights, dims[dim] // shards_of).reshape([-1 if axis == dim else 1 for axis in range(len(dims))])
    return gain


def normal_values(rng, dims, width, reach, cuts=(), kind=jnp.bfloat16):
    values = jax.random.normal(rng, dims, jnp.float32) * width
    if len(cuts) > 0:
        values = steps_of(rng, dims, cuts, -0.22, 0.18) * values
    return jnp.clip(values, min=-reach, max=reach).astype(kind)


def setup_inputs(seed: int = 0) -> dict:
    key_list = jax.random.split(jax.random.key(seed), 10)
    lin_q = normal_values(key_list[0], (SEQ, HEADS * HD), 1.0, 6.0, ((0, 8), (1, 4)))
    lin_k = normal_values(key_list[1], (SEQ, HEADS * HD), 1.0, 6.0, ((0, 8), (1, 4)))
    lin_v = draw_lin_v(jax.random.fold_in(key_list[9], 71), 0)
    att_q = draw_att_q(jax.random.fold_in(key_list[9], 71), 0)
    att_k = draw_att_k(jax.random.fold_in(key_list[9], 71), 0)
    att_v = draw_att_v(jax.random.fold_in(key_list[9], 71), 0)
    block_lists = draw_block_lists(jax.random.fold_in(key_list[9], 71), 0)
    gain_lin = jnp.clip(1.0 + 0.15 * jax.random.normal(key_list[7], (HEADS * HD,), jnp.float32), 0.25, 1.75).astype(jnp.bfloat16)
    gain_att = jnp.clip(1.0 + 0.15 * jax.random.normal(key_list[8], (HEADS * HD,), jnp.float32), 0.25, 1.75).astype(jnp.bfloat16)
    return {"lin_q": lin_q, "lin_k": lin_k, "lin_v": lin_v, "att_q": att_q, "att_k": att_k, "att_v": att_v, "block_lists": block_lists, "gain_lin": gain_lin, "gain_att": gain_att}


epsilon = 1e-06

def linear_mixer(lin_q, lin_k, lin_v):
    query_blocks = lin_q.reshape(NBLK, BLK, HEADS, HD)
    key_blocks = lin_k.reshape(NBLK, BLK, HEADS, HD)
    value_blocks = lin_v.reshape(NBLK, BLK, HEADS, HD)
    lower = jnp.arange(BLK)[:, None] >= jnp.arange(BLK)[None, :]

    def advance(state, pieces):
        query_blk = pieces[0].astype(jnp.float32)
        key_blk = pieces[1].astype(jnp.float32)
        value_blk = pieces[2].astype(jnp.float32)
        scores = jnp.einsum('thd,shd->hts', query_blk, key_blk)
        scores = lax.optimization_barrier(jnp.where(lower[None], scores, 0.0).astype(jnp.bfloat16))
        intra = jnp.einsum('hts,shd->thd', scores.astype(jnp.float32), value_blk)
        carried_low = lax.optimization_barrier(state.astype(jnp.bfloat16))
        inter = jnp.einsum('thd,hde->the', query_blk, carried_low.astype(jnp.float32))
        state = state + jnp.einsum('shd,she->hde', key_blk, value_blk)
        return (state, intra + inter)
    initial = jnp.zeros((HEADS, HD, HD), jnp.float32)
    final_state, outputs = lax.scan(advance, initial, (query_blocks, key_blocks, value_blocks))
    return outputs.reshape(SEQ, HEADS * HD)

def tree_attention(att_q, att_k, att_v, block_lists):
    groups = HEADS // KV_HEADS
    score_scale = HD ** (-0.5)
    padding = jnp.zeros(((SPAN - 1) * BLK, KV_HEADS * HD), att_k.dtype)
    keys_padded = jnp.concatenate([padding, att_k], axis=0)
    values_padded = jnp.concatenate([padding, att_v], axis=0)

    def one_block(block):
        start = (block * BLK).astype(jnp.int32)
        queries = lax.dynamic_slice_in_dim(att_q, start, BLK, 0).astype(jnp.float32).reshape(BLK, KV_HEADS, groups, HD)
        keys_win = lax.dynamic_slice_in_dim(keys_padded, start, SPAN * BLK, 0).astype(jnp.float32).reshape(SPAN * BLK, KV_HEADS, HD)
        values_win = lax.dynamic_slice_in_dim(values_padded, start, SPAN * BLK, 0).astype(jnp.float32).reshape(SPAN * BLK, KV_HEADS, HD)
        key_index = jnp.arange(SPAN * BLK, dtype=jnp.int32)
        key_block = block - (SPAN - 1) + key_index // BLK
        entries = block_lists[block]
        listed = jnp.any(entries[None, :] == key_block[:, None], axis=1) & (key_block >= 0)
        query_pos = block * BLK + jnp.arange(BLK, dtype=jnp.int32)
        key_pos = (block - (SPAN - 1)) * BLK + key_index
        allowed = listed[None, :] & (key_pos[None, :] <= query_pos[:, None])
        scores = jnp.einsum('tgqd,sgd->gqts', queries, keys_win) * score_scale
        scores = jnp.where(allowed[None, None], scores, -1e+30)
        row_max = lax.optimization_barrier(jnp.max(scores, axis=-1, keepdims=True))
        expo = jnp.exp(scores - row_max)
        weights = (expo / lax.optimization_barrier(jnp.sum(expo, axis=-1, keepdims=True))).astype(jnp.bfloat16)
        attended = jnp.einsum('gqts,sgd->tgqd', weights.astype(jnp.float32), values_win)
        return attended.reshape(BLK, HEADS * HD)
    outputs = lax.map(one_block, jnp.arange(NBLK, dtype=jnp.int32))
    return outputs.reshape(SEQ, HEADS * HD)

def reference(lin_q, lin_k, lin_v, att_q, att_k, att_v, block_lists, gain_lin, gain_att):
    lin_out = linear_mixer(lin_q, lin_k, lin_v)
    att_out = tree_attention(att_q, att_k, att_v, block_lists)
    lin_norm = lin_out / jnp.sqrt(lax.optimization_barrier(jnp.mean(lin_out * lin_out, axis=1, keepdims=True)) + epsilon)
    att_norm = att_out / jnp.sqrt(lax.optimization_barrier(jnp.mean(att_out * att_out, axis=1, keepdims=True)) + epsilon)
    mixed = lin_norm * gain_lin.astype(jnp.float32)[None, :] + att_norm * gain_att.astype(jnp.float32)[None, :]
    return mixed.astype(jnp.bfloat16)
```

```python
import functools
import math

import jax
import jax.numpy as jnp
from jax import lax
from jax.experimental import pallas as pl
from jax.experimental.pallas import tpu as pltpu
from jax.sharding import PartitionSpec as P

HD = 128
BLK = 128
SPAN = 5
EPS = 1e-06
NEG = -1e30
MESH = pl.DeviceIdType.MESH
BF16, F32 = jnp.bfloat16, jnp.float32

SIDE = BF16
CHAIN = F32
BACK = BF16


def dot(a, b, dims):
    return lax.dot_general(a, b, (dims, ((), ())), preferred_element_type=F32)


def kernel(
    n, nt, lists, lin_q_h, lin_k_h, lin_v_h, att_q_h, att_k_h, att_v_h, gains, out,
    lin_q, lin_k, lin_v, att_q, att_k, att_v, kv, total, first, scores, lin_out, att_out,
    xout, xin, zout, zin, bout, bin_, sq_out, sq_in,
    lsem, kvs, kvr, xs, xr, zs, zr, bs, br, ns, nr,
):
    ctx, tp = lax.axis_index("ctx"), lax.axis_index("tp")
    p, o = lax.rem(ctx, 2), lax.div(ctx, 2)
    mate = ctx + 1 - 2 * p
    tokens = lin_q.shape[0]
    heads = lin_q.shape[1] // HD
    kv_heads = att_k.shape[1] // HD
    half = heads // 2
    has_prev, has_next = o > 0, o < n // 2 - 1
    side, ahead, behind = {"ctx": mate}, {"ctx": ctx + 2}, {"ctx": ctx - 2}

    pairs = (
        (lin_k_h, lin_k), (lin_v_h, lin_v), (lin_q_h, lin_q),
        (att_q_h, att_q), (att_k_h, att_k), (att_v_h, att_v),
    )
    local = [pltpu.make_async_copy(s, d, lsem.at[i]) for i, (s, d) in enumerate(pairs)]
    for c in local:
        c.start()

    barrier = pltpu.get_barrier_semaphore()

    def greet(where):
        pl.semaphore_signal(barrier, inc=1, device_id=where, device_id_type=MESH)

    greet(side)
    for k in range(1, nt):
        greet({"tp": lax.rem(tp + k, nt)})
    pl.when(has_prev)(lambda: greet(behind))
    pl.when(has_next)(lambda: greet(ahead))
    pl.semaphore_wait(barrier, nt + has_prev.astype(jnp.int32) + has_next.astype(jnp.int32))

    def remote(src, dst, ssem, rsem, where):
        return pltpu.make_async_remote_copy(
            src_ref=src, dst_ref=dst, send_sem=ssem, recv_sem=rsem,
            device_id=where, device_id_type=MESH,
        )

    kv_src = (att_k_h, att_v_h)
    kv_ahead = [remote(kv_src[a], kv.at[1, a], kvs.at[a], kvr.at[a], ahead) for a in range(2)]
    kv_side = [remote(kv_src[a], kv.at[0, a], kvs.at[2 + a], kvr.at[2 + a], side) for a in range(2)]
    kv_pass = [remote(kv.at[1, a], kv.at[0, a], kvs.at[2 + a], kvr.at[2 + a], side) for a in range(2)]
    for a in range(2):
        pl.when(has_next)(kv_ahead[a].start)
        pl.when(p == 0)(kv_side[a].start)

    @pl.when(jnp.logical_not(has_prev))
    def _():
        kv[1] = jnp.zeros_like(kv[1])

        @pl.when(p == 0)
        def _():
            kv[0] = jnp.zeros_like(kv[0])

    local[0].wait()
    local[1].wait()

    def lanes(h):
        return pl.ds(pl.multiple_of(h * HD, HD), HD)

    x_copy = [remote(xout.at[j], xin.at[j], xs.at[j], xr.at[j], side) for j in range(half)]
    z_copy = [remote(zout.at[j], zin.at[j], zs.at[j], zr.at[j], ahead) for j in range(half)]
    b_copy = [remote(bout.at[j], bin_.at[j], bs.at[j], br.at[j], side) for j in range(half)]
    other, mine = (1 - p) * half, p * half

    for j in range(half):
        h = other + j
        xout[j] = dot(lin_k[:, lanes(h)], lin_v[:, lanes(h)], ((0,), (0,))).astype(SIDE)
        x_copy[j].start()
    for j in range(half):
        h = mine + j
        total[j] = dot(lin_k[:, lanes(h)], lin_v[:, lanes(h)], ((0,), (0,)))

    local[2].wait()
    row = lax.broadcasted_iota(jnp.int32, (BLK, BLK), 0)
    col = lax.broadcasted_iota(jnp.int32, (BLK, BLK), 1)
    lower = row >= col
    blocks = tokens // BLK
    for h in range(heads):
        hs = pl.ds(h * HD, HD)
        for b in range(blocks):
            rows = pl.ds(b * BLK, BLK)
            s = dot(lin_q[rows, hs], lin_k[rows, hs], ((1,), (1,)))
            scores[rows, hs] = jnp.where(lower, s, 0.0).astype(BF16)
        first[h] = dot(lin_k[0:BLK, hs], lin_v[0:BLK, hs], ((0,), (0,)))

    for a in range(2):
        @pl.when(has_prev)
        def _():
            kv_ahead[a].wait_recv()

            @pl.when(p == 1)
            def _():
                kv_pass[a].start()

    for j in range(half):
        @pl.when(has_prev)
        def _():
            z_copy[j].wait_recv()

        @pl.when(jnp.logical_not(has_prev))
        def _():
            zin[j] = jnp.zeros_like(zin[j])

        x_copy[j].wait_recv()
        before = zin[j].astype(F32)
        here, there = total[j], xin[j].astype(F32)
        zout[j] = (before + here + there).astype(CHAIN)
        pl.when(has_next)(z_copy[j].start)
        bout[j] = jnp.where(p == 0, before + here, before).astype(BACK)
        b_copy[j].start()
        total[j] = jnp.where(p == 0, before, before + there)

    for c in local[3:]:
        c.wait()
    for a in range(2):
        @pl.when((p == 1) | has_prev)
        def _():
            kv_side[a].wait_recv()

    factor = (HD ** -0.5) * math.log2(math.e)
    att_sq = [None] * blocks
    for b in range(blocks):
        rows = pl.ds(b * BLK, BLK)
        block = ctx * blocks + b
        bias = []
        for i in range(SPAN - 1):
            key_block = block - (SPAN - 1) + i
            hit = lists[b, 0] == key_block
            for e in range(1, 4):
                hit = hit | (lists[b, e] == key_block)
            bias.append(jnp.where(hit & (key_block >= 0), 0.0, NEG).astype(F32))
        bias_row = jnp.concatenate([jnp.full((1, BLK), v, F32) for v in bias], axis=1)

        def window(a, own, hs):
            parts = [kv[1, a, b * BLK:, hs], kv[0, a, :, hs], own[: (b + 1) * BLK, hs]]
            return jnp.concatenate(parts, axis=0)

        for g in range(kv_heads):
            gs = pl.ds(g * HD, HD)
            keys, values = window(0, att_k, gs), window(1, att_v, gs)
            for h in range(g * heads // kv_heads, (g + 1) * heads // kv_heads):
                hs = pl.ds(h * HD, HD)
                s = dot(att_q[rows, hs], keys, ((1,), (1,)))
                cut = (SPAN - 1) * BLK
                s = jnp.concatenate(
                    [s[:, :cut] + bias_row, jnp.where(lower, s[:, cut:], NEG)], axis=1
                )
                e = jnp.exp2((s - jnp.max(s, axis=1, keepdims=True)) * factor)
                w = (e * (1.0 / jnp.sum(e, axis=1, keepdims=True))).astype(BF16)
                r = dot(w, values, ((1,), (0,)))
                att_out[rows, hs] = r
                att_sq[b] = r * r if att_sq[b] is None else att_sq[b] + r * r

    lin_sq = [None] * blocks

    def finish(h, prefix):
        for b in range(blocks):
            rows = pl.ds(b * BLK, BLK)
            low = (prefix if b == 0 else prefix + first[h]).astype(BF16)
            lhs = jnp.concatenate([scores[rows, lanes(h)], lin_q[rows, lanes(h)]], axis=1)
            rhs = jnp.concatenate([lin_v[rows, lanes(h)], low], axis=0)
            r = dot(lhs, rhs, ((1,), (0,)))
            lin_out[rows, lanes(h)] = r
            lin_sq[b] = r * r if lin_sq[b] is None else lin_sq[b] + r * r

    for j in range(half):
        finish(mine + j, total[j])
    for j in range(half):
        b_copy[j].wait_recv()
        finish(other + j, bin_[j].astype(F32))

    def as_row(parts):
        return jnp.sum(jnp.concatenate(parts, axis=0).T, axis=0, keepdims=True)

    top = lax.broadcasted_iota(jnp.int32, (8, tokens), 0) == 0
    sums = jnp.where(top, as_row(lin_sq), as_row(att_sq))
    sq_out[...] = sums
    n_copy = [
        remote(sq_out, sq_in.at[k - 1], ns.at[k - 1], nr.at[k - 1], {"tp": lax.rem(tp + k, nt)})
        for k in range(1, nt)
    ]
    for c in n_copy:
        c.start()
    for a in range(2):
        pl.when(has_next)(kv_ahead[a].wait_send)
        pl.when((p == 0) | has_prev)(kv_side[a].wait_send)
    for j in range(half):
        x_copy[j].wait_send()
        pl.when(has_next)(z_copy[j].wait_send)
        b_copy[j].wait_send()
    for k in range(nt - 1):
        n_copy[k].wait_recv()
        sums = sums + sq_in[k]
    inv = lax.rsqrt(sums * (1.0 / (nt * heads * HD)) + EPS)

    def as_column(r):
        return jnp.broadcast_to(r, (HD, tokens)).T

    lin_inv, att_inv = as_column(inv[0:1]), as_column(inv[1:2])
    for h in range(heads):
        hs = pl.ds(h * HD, HD)
        out[:, hs] = (
            lin_out[:, hs] * lin_inv * gains[0:1, hs] + att_out[:, hs] * att_inv * gains[1:2, hs]
        ).astype(BF16)
    for c in n_copy:
        c.wait_send()


def per_device(n, nt, lin_q, lin_k, lin_v, att_q, att_k, att_v, block_lists, gain_lin, gain_att):
    tokens, columns = lin_q.shape
    heads, half = columns // HD, columns // HD // 2
    gains = jnp.stack([gain_lin, gain_att]).astype(F32)
    anywhere = pl.BlockSpec(memory_space=pl.ANY)
    vmem = pl.BlockSpec(memory_space=pltpu.VMEM)
    wide, kv_wide = (tokens, columns), att_k.shape
    state = (half, HD, HD)
    dma = pltpu.SemaphoreType.DMA
    return pl.pallas_call(
        functools.partial(kernel, n, nt),
        out_shape=jax.ShapeDtypeStruct(wide, BF16),
        in_specs=[pl.BlockSpec(memory_space=pltpu.SMEM)] + [anywhere] * 6 + [vmem],
        out_specs=vmem,
        scratch_shapes=[
            pltpu.VMEM(wide, BF16), pltpu.VMEM(wide, BF16), pltpu.VMEM(wide, BF16),
            pltpu.VMEM(wide, BF16), pltpu.VMEM(kv_wide, BF16), pltpu.VMEM(kv_wide, BF16),
            pltpu.VMEM((2, 2) + kv_wide, BF16),
            pltpu.VMEM(state, F32), pltpu.VMEM((heads, HD, HD), F32),
            pltpu.VMEM(wide, BF16), pltpu.VMEM(wide, F32), pltpu.VMEM(wide, F32),
            pltpu.VMEM(state, SIDE), pltpu.VMEM(state, SIDE),
            pltpu.VMEM(state, CHAIN), pltpu.VMEM(state, CHAIN),
            pltpu.VMEM(state, BACK), pltpu.VMEM(state, BACK),
            pltpu.VMEM((8, tokens), F32), pltpu.VMEM((nt - 1, 8, tokens), F32),
            dma((6,)), dma((4,)), dma((4,)),
            dma((half,)), dma((half,)), dma((half,)), dma((half,)), dma((half,)), dma((half,)),
            dma((nt - 1,)), dma((nt - 1,)),
        ],
        compiler_params=pltpu.CompilerParams(
            collective_id=0, has_side_effects=True, vmem_limit_bytes=48 * 2 ** 20
        ),
    )(block_lists, lin_q, lin_k, lin_v, att_q, att_k, att_v, gains)


def solution(mesh):
    wide = P("ctx", "tp")
    return jax.shard_map(
        functools.partial(per_device, mesh.shape["ctx"], mesh.shape["tp"]),
        mesh=mesh,
        in_specs=(wide,) * 6 + (P("ctx", None), P("tp"), P("tp")),
        out_specs=wide,
        check_vma=False,
    )
```

```python
import functools
import math

import jax
import jax.numpy as jnp
from jax import lax
from jax.experimental import pallas as pl
from jax.experimental.pallas import tpu as pltpu
from jax.sharding import PartitionSpec as P

HD = 128
BLK = 128
SPAN = 5
EPS = 1e-06
NEG = -1e30
MESH = pl.DeviceIdType.MESH
BF16, F32 = jnp.bfloat16, jnp.float32

SIDE = BF16
CHAIN = BF16
BACK = BF16


def dot(a, b, dims):
    return lax.dot_general(a, b, (dims, ((), ())), preferred_element_type=F32)


def kernel(
    n, nt, lists, lin_q_h, lin_k_h, lin_v_h, att_q_h, att_k_h, att_v_h, gain_lin_h, gain_att_h,
    out, lin_q, lin_k, lin_v, att_q, att_k, att_v, gain_lin, gain_att, kv, total, first, scores, lin_out, att_out,
    xout, xin, zout, zin, bout, bin_, sq_out, sq_in,
    lsem, kvs, kvr, xs, xr, zs, zr, bs, br, ns, nr,
):
    ctx, tp = lax.axis_index("ctx"), lax.axis_index("tp")
    p, o = lax.rem(ctx, 2), lax.div(ctx, 2)
    mate = ctx + 1 - 2 * p
    tokens = lin_q.shape[0]
    heads = lin_q.shape[1] // HD
    kv_heads = att_k.shape[1] // HD
    half = heads // 2
    has_prev, has_next = o > 0, o < n // 2 - 1
    side, ahead, behind = {"ctx": mate}, {"ctx": ctx + 2}, {"ctx": ctx - 2}

    pairs = (
        (lin_k_h, lin_k), (lin_v_h, lin_v), (lin_q_h, lin_q),
        (att_q_h, att_q), (att_k_h, att_k), (att_v_h, att_v),
        (gain_lin_h, gain_lin), (gain_att_h, gain_att),
    )
    local = [pltpu.make_async_copy(s, d, lsem.at[i]) for i, (s, d) in enumerate(pairs)]
    for c in local:
        c.start()

    barrier = pltpu.get_barrier_semaphore()

    def greet(where):
        pl.semaphore_signal(barrier, inc=1, device_id=where, device_id_type=MESH)

    greet(side)
    for k in range(1, nt):
        greet({"tp": lax.rem(tp + k, nt)})
    pl.when(has_prev)(lambda: greet(behind))
    pl.when(has_next)(lambda: greet(ahead))
    pl.semaphore_wait(barrier, nt + has_prev.astype(jnp.int32) + has_next.astype(jnp.int32))

    def remote(src, dst, ssem, rsem, where):
        return pltpu.make_async_remote_copy(
            src_ref=src, dst_ref=dst, send_sem=ssem, recv_sem=rsem,
            device_id=where, device_id_type=MESH,
        )

    def kv_copies(src, slot, sem, where):
        return [
            [
                remote(
                    src[a].at[:, pl.ds(g * HD, HD)], kv.at[slot, a, :, pl.ds(g * HD, HD)],
                    kvs.at[sem, g, a], kvr.at[sem, g, a], where,
                )
                for a in range(2)
            ]
            for g in range(kv_heads)
        ]

    kv_src = (att_k_h, att_v_h)
    kv_ahead = kv_copies(kv_src, 1, 1, ahead)
    kv_side = kv_copies(kv_src, 0, 0, side)
    kv_pass = kv_copies((kv.at[1, 0], kv.at[1, 1]), 0, 0, side)

    def send_kv(g):
        for a in range(2):
            pl.when(has_next)(kv_ahead[g][a].start)
            pl.when(p == 0)(kv_side[g][a].start)

    def sent_kv(g):
        for a in range(2):
            pl.when(has_next)(kv_ahead[g][a].wait_send)
            pl.when(p == 0)(kv_side[g][a].wait_send)

    send_kv(0)

    @pl.when(jnp.logical_not(has_prev))
    def _():
        kv[1] = jnp.zeros_like(kv[1])

        @pl.when(p == 0)
        def _():
            kv[0] = jnp.zeros_like(kv[0])

    local[0].wait()
    local[1].wait()

    def lanes(h):
        return pl.ds(pl.multiple_of(h * HD, HD), HD)

    x_copy = [remote(xout.at[j], xin.at[j], xs.at[j], xr.at[j], side) for j in range(half)]
    z_copy = [remote(zout.at[j], zin.at[j], zs.at[j], zr.at[j], ahead) for j in range(half)]
    b_copy = [remote(bout.at[j], bin_.at[j], bs.at[j], br.at[j], side) for j in range(half)]
    other, mine = (1 - p) * half, p * half

    for j in range(half):
        h = other + j
        xout[j] = dot(lin_k[:, lanes(h)], lin_v[:, lanes(h)], ((0,), (0,))).astype(SIDE)
        x_copy[j].start()
    for g in range(1, kv_heads):
        sent_kv(g - 1)
        send_kv(g)
    for j in range(half):
        h = mine + j
        total[j] = dot(lin_k[:, lanes(h)], lin_v[:, lanes(h)], ((0,), (0,)))

    local[2].wait()
    row = lax.broadcasted_iota(jnp.int32, (BLK, BLK), 0)
    col = lax.broadcasted_iota(jnp.int32, (BLK, BLK), 1)
    lower = row >= col
    blocks = tokens // BLK
    for h in range(heads):
        hs = pl.ds(h * HD, HD)
        for b in range(blocks):
            rows = pl.ds(b * BLK, BLK)
            s = dot(lin_q[rows, hs], lin_k[rows, hs], ((1,), (1,)))
            scores[rows, hs] = jnp.where(lower, s, 0.0).astype(BF16)
        first[h] = dot(lin_k[0:BLK, hs], lin_v[0:BLK, hs], ((0,), (0,)))

    def forward(g):
        @pl.when(has_prev)
        def _():
            for a in range(2):
                kv_ahead[g][a].wait_recv()

                @pl.when(p == 1)
                def _():
                    kv_pass[g][a].start()

    def chain():
        for j in range(half):
            @pl.when(has_prev)
            def _():
                z_copy[j].wait_recv()

            @pl.when(jnp.logical_not(has_prev))
            def _():
                zin[j] = jnp.zeros_like(zin[j])

            x_copy[j].wait_recv()
            before = zin[j].astype(F32)
            here, there = total[j], xin[j].astype(F32)
            zout[j] = (before + here + there).astype(CHAIN)
            pl.when(has_next)(z_copy[j].start)
            bout[j] = jnp.where(p == 0, before + here, before).astype(BACK)
            b_copy[j].start()
            total[j] = jnp.where(p == 0, before, before + there)

    for g in range(kv_heads):
        forward(g)
    early = has_next & (o < 2)
    middle = has_next & (o >= 2)
    late = jnp.logical_not(has_next)
    pl.when(early)(chain)
    for c in local[3:]:
        c.wait()
    factor = (HD ** -0.5) * math.log2(math.e)
    cut = (SPAN - 1) * BLK
    bias = []
    for b in range(blocks):
        parts = []
        for i in range(SPAN - 1):
            key_block = ctx * blocks + b - (SPAN - 1) + i
            hit = lists[b, 0] == key_block
            for e in range(1, 4):
                hit = hit | (lists[b, e] == key_block)
            value = jnp.where(hit & (key_block >= 0), 0.0, NEG).astype(F32)
            parts.append(jnp.full((1, BLK), value, F32))
        bias.append(jnp.concatenate(parts, axis=1))

    att_sq = [None] * blocks

    def attend(g):
        gs = pl.ds(g * HD, HD)
        for a in range(2):
            @pl.when((p == 1) | has_prev)
            def _():
                kv_side[g][a].wait_recv()

        for b in range(blocks):
            rows = pl.ds(b * BLK, BLK)

            def window(a, own):
                parts = [kv[1, a, b * BLK:, gs], kv[0, a, :, gs], own[: (b + 1) * BLK, gs]]
                return jnp.concatenate(parts, axis=0)

            keys, values = window(0, att_k), window(1, att_v)
            for h in range(g * heads // kv_heads, (g + 1) * heads // kv_heads):
                hs = pl.ds(h * HD, HD)
                s = dot(att_q[rows, hs], keys, ((1,), (1,)))
                s = jnp.concatenate(
                    [s[:, :cut] + bias[b], jnp.where(lower, s[:, cut:], NEG)], axis=1
                )
                e = jnp.exp2((s - jnp.max(s, axis=1, keepdims=True)) * factor)
                w = (e * (1.0 / jnp.sum(e, axis=1, keepdims=True))).astype(BF16)
                r = dot(w, values, ((1,), (0,)))
                att_out[rows, hs] = r
                att_sq[b] = r * r if att_sq[b] is None else att_sq[b] + r * r

    for g in range(kv_heads):
        attend(g)
        if g == 0:
            pl.when(middle)(chain)
    pl.when(late)(chain)
    lin_sq = [None] * blocks

    def finish(h, prefix):
        for b in range(blocks):
            rows = pl.ds(b * BLK, BLK)
            low = (prefix if b == 0 else prefix + first[h]).astype(BF16)
            lhs = jnp.concatenate([scores[rows, lanes(h)], lin_q[rows, lanes(h)]], axis=1)
            rhs = jnp.concatenate([lin_v[rows, lanes(h)], low], axis=0)
            r = dot(lhs, rhs, ((1,), (0,)))
            lin_out[rows, lanes(h)] = r
            lin_sq[b] = r * r if lin_sq[b] is None else lin_sq[b] + r * r

    for j in range(half):
        finish(mine + j, total[j])
    for j in range(half):
        b_copy[j].wait_recv()
        finish(other + j, bin_[j].astype(F32))

    def as_row(parts):
        return jnp.sum(jnp.concatenate(parts, axis=0).T, axis=0, keepdims=True)

    top = lax.broadcasted_iota(jnp.int32, (8, tokens), 0) == 0
    sums = jnp.where(top, as_row(lin_sq), as_row(att_sq))
    sq_out[...] = sums
    n_copy = [
        remote(sq_out, sq_in.at[k - 1], ns.at[k - 1], nr.at[k - 1], {"tp": lax.rem(tp + k, nt)})
        for k in range(1, nt)
    ]
    for c in n_copy:
        c.start()
    sent_kv(kv_heads - 1)
    @pl.when((p == 1) & has_prev)
    def _():
        for g in range(kv_heads):
            for a in range(2):
                kv_pass[g][a].wait_send()
    for j in range(half):
        x_copy[j].wait_send()
        pl.when(has_next)(z_copy[j].wait_send)
        b_copy[j].wait_send()
    for k in range(nt - 1):
        n_copy[k].wait_recv()
        sums = sums + sq_in[k]
    inv = lax.rsqrt(sums * (1.0 / (nt * heads * HD)) + EPS)

    def as_column(r):
        return jnp.broadcast_to(r, (HD, tokens)).T

    lin_inv, att_inv = as_column(inv[0:1]), as_column(inv[1:2])
    for h in range(heads):
        hs = pl.ds(h * HD, HD)
        out[:, hs] = (
            lin_out[:, hs] * lin_inv * gain_lin[:, hs].astype(F32) + att_out[:, hs] * att_inv * gain_att[:, hs].astype(F32)
        ).astype(BF16)
    for c in n_copy:
        c.wait_send()


def per_device(n, nt, lin_q, lin_k, lin_v, att_q, att_k, att_v, block_lists, gain_lin, gain_att):
    tokens, columns = lin_q.shape
    heads, half = columns // HD, columns // HD // 2
    gain_lin, gain_att = gain_lin.reshape(1, columns), gain_att.reshape(1, columns)
    anywhere = pl.BlockSpec(memory_space=pl.ANY)
    wide, kv_wide = (tokens, columns), att_k.shape
    state, kv_heads = (half, HD, HD), kv_wide[1] // HD
    dma = pltpu.SemaphoreType.DMA
    return pl.pallas_call(
        functools.partial(kernel, n, nt),
        out_shape=jax.ShapeDtypeStruct(wide, BF16),
        in_specs=[pl.BlockSpec(memory_space=pltpu.SMEM)] + [anywhere] * 8,
        out_specs=pl.BlockSpec(memory_space=pltpu.VMEM),
        scratch_shapes=[
            pltpu.VMEM(wide, BF16), pltpu.VMEM(wide, BF16), pltpu.VMEM(wide, BF16),
            pltpu.VMEM(wide, BF16), pltpu.VMEM(kv_wide, BF16), pltpu.VMEM(kv_wide, BF16),
            pltpu.VMEM((1, columns), BF16), pltpu.VMEM((1, columns), BF16),
            pltpu.VMEM((2, 2) + kv_wide, BF16),
            pltpu.VMEM(state, F32), pltpu.VMEM((heads, HD, HD), F32),
            pltpu.VMEM(wide, BF16), pltpu.VMEM(wide, F32), pltpu.VMEM(wide, F32),
            pltpu.VMEM(state, SIDE), pltpu.VMEM(state, SIDE),
            pltpu.VMEM(state, CHAIN), pltpu.VMEM(state, CHAIN),
            pltpu.VMEM(state, BACK), pltpu.VMEM(state, BACK),
            pltpu.VMEM((8, tokens), F32), pltpu.VMEM((nt - 1, 8, tokens), F32),
            dma((8,)), dma((2, kv_heads, 2)), dma((2, kv_heads, 2)),
            dma((half,)), dma((half,)), dma((half,)), dma((half,)), dma((half,)), dma((half,)),
            dma((nt - 1,)), dma((nt - 1,)),
        ],
        compiler_params=pltpu.CompilerParams(
            collective_id=0, has_side_effects=True, vmem_limit_bytes=63 * 2 ** 20
        ),
    )(block_lists, lin_q, lin_k, lin_v, att_q, att_k, att_v, gain_lin, gain_att)


def solution(mesh):
    wide = P("ctx", "tp")
    return jax.shard_map(
        functools.partial(per_device, mesh.shape["ctx"], mesh.shape["tp"]),
        mesh=mesh,
        in_specs=(wide,) * 6 + (P("ctx", None), P("tp"), P("tp")),
        out_specs=wide,
        check_vma=False,
    )
```

```python
import functools
import math

import jax
import jax.numpy as jnp
from jax import lax
from jax.experimental import pallas as pl
from jax.experimental.pallas import tpu as pltpu
from jax.sharding import PartitionSpec as P

HD = 128
BLK = 128
SPAN = 5
EPS = 1e-06
NEG = -1e30
MESH = pl.DeviceIdType.MESH
BF16, F32 = jnp.bfloat16, jnp.float32

SIDE = BF16
CHAIN = BF16
BACK = BF16


def dot(a, b, dims):
    return lax.dot_general(a, b, (dims, ((), ())), preferred_element_type=F32)


def kernel(
    n, nt, lists, lin_q_h, lin_k_h, lin_v_h, att_q_h, att_k_h, att_v_h, gain_lin_h, gain_att_h,
    out, lin_q, lin_k, lin_v, att_q, att_k, att_v, gain_lin, gain_att, kv, total, first, scores, lin_out, att_out,
    xout, xin, zout, zin, bout, bin_, sq_out, sq_in,
    lsem, kvs, kvr, xs, xr, zs, zr, bs, br, ns, nr,
):
    ctx, tp = lax.axis_index("ctx"), lax.axis_index("tp")
    p, o = lax.rem(ctx, 2), lax.div(ctx, 2)
    mate = ctx + 1 - 2 * p
    tokens = lin_q.shape[0]
    heads = lin_q.shape[1] // HD
    kv_heads = att_k.shape[1] // HD
    half = heads // 2
    has_prev, has_next = o > 0, o < n // 2 - 1
    side, ahead, behind = {"ctx": mate}, {"ctx": ctx + 2}, {"ctx": ctx - 2}

    pairs = (
        (lin_k_h, lin_k), (lin_v_h, lin_v), (lin_q_h, lin_q),
        (att_q_h, att_q), (att_k_h, att_k), (att_v_h, att_v),
        (gain_lin_h, gain_lin), (gain_att_h, gain_att),
    )
    local = [pltpu.make_async_copy(s, d, lsem.at[i]) for i, (s, d) in enumerate(pairs)]
    for c in local:
        c.start()

    barrier = pltpu.get_barrier_semaphore()

    def greet(where):
        pl.semaphore_signal(barrier, inc=1, device_id=where, device_id_type=MESH)

    greet(side)
    for k in range(1, nt):
        greet({"tp": lax.rem(tp + k, nt)})
    pl.when(has_prev)(lambda: greet(behind))
    pl.when(has_next)(lambda: greet(ahead))
    pl.semaphore_wait(barrier, nt + has_prev.astype(jnp.int32) + has_next.astype(jnp.int32))

    def remote(src, dst, ssem, rsem, where):
        return pltpu.make_async_remote_copy(
            src_ref=src, dst_ref=dst, send_sem=ssem, recv_sem=rsem,
            device_id=where, device_id_type=MESH,
        )

    def kv_copies(src, slot, sem, where):
        return [
            [
                remote(
                    src[a].at[:, pl.ds(g * HD, HD)], kv.at[slot, a, :, pl.ds(g * HD, HD)],
                    kvs.at[sem, g, a], kvr.at[sem, g, a], where,
                )
                for a in range(2)
            ]
            for g in range(kv_heads)
        ]

    kv_src = (att_k_h, att_v_h)
    kv_ahead = kv_copies(kv_src, 1, 1, ahead)
    kv_side = kv_copies(kv_src, 0, 0, side)
    kv_pass = kv_copies((kv.at[1, 0], kv.at[1, 1]), 0, 0, side)

    def send_kv(g):
        for a in range(2):
            pl.when(has_next)(kv_ahead[g][a].start)
            pl.when(p == 0)(kv_side[g][a].start)

    def sent_kv(g):
        for a in range(2):
            pl.when(has_next)(kv_ahead[g][a].wait_send)
            pl.when(p == 0)(kv_side[g][a].wait_send)

    send_kv(0)

    @pl.when(jnp.logical_not(has_prev))
    def _():
        kv[1] = jnp.zeros_like(kv[1])

        @pl.when(p == 0)
        def _():
            kv[0] = jnp.zeros_like(kv[0])

    local[0].wait()
    local[1].wait()

    def lanes(h):
        return pl.ds(pl.multiple_of(h * HD, HD), HD)

    x_copy = [remote(xout.at[j], xin.at[j], xs.at[j], xr.at[j], side) for j in range(half)]
    z_copy = [remote(zout.at[j], zin.at[j], zs.at[j], zr.at[j], ahead) for j in range(half)]
    b_copy = [remote(bout.at[j], bin_.at[j], bs.at[j], br.at[j], side) for j in range(half)]
    other, mine = (1 - p) * half, p * half

    for j in range(half):
        h = other + j
        xout[j] = dot(lin_k[:, lanes(h)], lin_v[:, lanes(h)], ((0,), (0,))).astype(SIDE)
        x_copy[j].start()
    for g in range(1, kv_heads):
        sent_kv(g - 1)
        send_kv(g)
    for j in range(half):
        h = mine + j
        total[j] = dot(lin_k[:, lanes(h)], lin_v[:, lanes(h)], ((0,), (0,)))

    local[2].wait()
    row = lax.broadcasted_iota(jnp.int32, (BLK, BLK), 0)
    col = lax.broadcasted_iota(jnp.int32, (BLK, BLK), 1)
    lower = row >= col
    blocks = tokens // BLK
    for h in range(heads):
        hs = pl.ds(h * HD, HD)
        for b in range(blocks):
            rows = pl.ds(b * BLK, BLK)
            s = dot(lin_q[rows, hs], lin_k[rows, hs], ((1,), (1,)))
            scores[rows, hs] = jnp.where(lower, s, 0.0).astype(BF16)
        first[h] = dot(lin_k[0:BLK, hs], lin_v[0:BLK, hs], ((0,), (0,)))

    def forward(g):
        @pl.when(has_prev)
        def _():
            for a in range(2):
                kv_ahead[g][a].wait_recv()

                @pl.when(p == 1)
                def _():
                    kv_pass[g][a].start()

    def chain():
        for j in range(half):
            @pl.when(has_prev)
            def _():
                z_copy[j].wait_recv()

            @pl.when(jnp.logical_not(has_prev))
            def _():
                zin[j] = jnp.zeros_like(zin[j])

            x_copy[j].wait_recv()
            before = zin[j].astype(F32)
            here, there = total[j], xin[j].astype(F32)
            zout[j] = (before + here + there).astype(CHAIN)
            pl.when(has_next)(z_copy[j].start)
            bout[j] = jnp.where(p == 0, before + here, before).astype(BACK)
            b_copy[j].start()
            total[j] = jnp.where(p == 0, before, before + there)

    for g in range(kv_heads):
        forward(g)
    early = has_next & (o < 2)
    middle = has_next & (o >= 2)
    late = jnp.logical_not(has_next)
    pl.when(early)(chain)
    for c in local[3:]:
        c.wait()
    factor = (HD ** -0.5) * math.log2(math.e)
    cut = (SPAN - 1) * BLK
    bias = []
    for b in range(blocks):
        parts = []
        for i in range(SPAN - 1):
            key_block = ctx * blocks + b - (SPAN - 1) + i
            hit = lists[b, 0] == key_block
            for e in range(1, 4):
                hit = hit | (lists[b, e] == key_block)
            value = jnp.where(hit & (key_block >= 0), 0.0, NEG).astype(F32)
            parts.append(jnp.full((1, BLK), value, F32))
        bias.append(jnp.concatenate(parts, axis=1))

    att_sq = [None] * blocks

    def attend(g):
        gs = pl.ds(g * HD, HD)
        for a in range(2):
            @pl.when((p == 1) | has_prev)
            def _():
                kv_side[g][a].wait_recv()

        for b in range(blocks):
            rows = pl.ds(b * BLK, BLK)

            def window(a, own):
                parts = [kv[1, a, b * BLK:, gs], kv[0, a, :, gs], own[: (b + 1) * BLK, gs]]
                return jnp.concatenate(parts, axis=0)

            keys, values = window(0, att_k), window(1, att_v)
            group = range(g * heads // kv_heads, (g + 1) * heads // kv_heads)
            queries = jnp.concatenate([att_q[rows, pl.ds(h * HD, HD)] for h in group], axis=0)
            sall = dot(queries, keys, ((1,), (1,)))
            wall = []
            for i in range(len(group)):
                s = sall[i * BLK:(i + 1) * BLK]
                s = jnp.concatenate(
                    [s[:, :cut] + bias[b], jnp.where(lower, s[:, cut:], NEG)], axis=1
                )
                e = jnp.exp2((s - jnp.max(s, axis=1, keepdims=True)) * factor)
                wall.append((e * (1.0 / jnp.sum(e, axis=1, keepdims=True))).astype(BF16))
            rall = dot(jnp.concatenate(wall, axis=0), values, ((1,), (0,)))
            for i, h in enumerate(group):
                r = rall[i * BLK:(i + 1) * BLK]
                att_out[rows, pl.ds(h * HD, HD)] = r
                att_sq[b] = r * r if att_sq[b] is None else att_sq[b] + r * r

    for g in range(kv_heads):
        attend(g)
        if g == 0:
            pl.when(middle)(chain)
    pl.when(late)(chain)
    lin_sq = [None] * blocks

    def finish(h, prefix):
        for b in range(blocks):
            rows = pl.ds(b * BLK, BLK)
            low = (prefix if b == 0 else prefix + first[h]).astype(BF16)
            lhs = jnp.concatenate([scores[rows, lanes(h)], lin_q[rows, lanes(h)]], axis=1)
            rhs = jnp.concatenate([lin_v[rows, lanes(h)], low], axis=0)
            r = dot(lhs, rhs, ((1,), (0,)))
            lin_out[rows, lanes(h)] = r
            lin_sq[b] = r * r if lin_sq[b] is None else lin_sq[b] + r * r

    for j in range(half):
        finish(mine + j, total[j])
    for j in range(half):
        b_copy[j].wait_recv()
        finish(other + j, bin_[j].astype(F32))

    def as_row(parts):
        return jnp.sum(jnp.concatenate(parts, axis=0).T, axis=0, keepdims=True)

    top = lax.broadcasted_iota(jnp.int32, (8, tokens), 0) == 0
    sums = jnp.where(top, as_row(lin_sq), as_row(att_sq))
    sq_out[...] = sums
    n_copy = [
        remote(sq_out, sq_in.at[k - 1], ns.at[k - 1], nr.at[k - 1], {"tp": lax.rem(tp + k, nt)})
        for k in range(1, nt)
    ]
    for c in n_copy:
        c.start()
    sent_kv(kv_heads - 1)
    @pl.when((p == 1) & has_prev)
    def _():
        for g in range(kv_heads):
            for a in range(2):
                kv_pass[g][a].wait_send()
    for j in range(half):
        x_copy[j].wait_send()
        pl.when(has_next)(z_copy[j].wait_send)
        b_copy[j].wait_send()
    for k in range(nt - 1):
        n_copy[k].wait_recv()
        sums = sums + sq_in[k]
    inv = lax.rsqrt(sums * (1.0 / (nt * heads * HD)) + EPS)

    def as_column(r):
        return jnp.broadcast_to(r, (HD, tokens)).T

    lin_inv, att_inv = as_column(inv[0:1]), as_column(inv[1:2])
    gl, ga = gain_lin[...].astype(F32), gain_att[...].astype(F32)
    for h in range(heads):
        hs = pl.ds(h * HD, HD)
        out[:, hs] = (
            lin_out[:, hs] * lin_inv * gl[h:h + 1] + att_out[:, hs] * att_inv * ga[h:h + 1]
        ).astype(BF16)
    for c in n_copy:
        c.wait_send()


def per_device(n, nt, lin_q, lin_k, lin_v, att_q, att_k, att_v, block_lists, gain_lin, gain_att):
    tokens, columns = lin_q.shape
    heads, half = columns // HD, columns // HD // 2
    gain_lin, gain_att = gain_lin.reshape(heads, HD), gain_att.reshape(heads, HD)
    anywhere = pl.BlockSpec(memory_space=pl.ANY)
    wide, kv_wide = (tokens, columns), att_k.shape
    state, kv_heads = (half, HD, HD), kv_wide[1] // HD
    dma = pltpu.SemaphoreType.DMA
    return pl.pallas_call(
        functools.partial(kernel, n, nt),
        out_shape=jax.ShapeDtypeStruct(wide, BF16),
        in_specs=[pl.BlockSpec(memory_space=pltpu.SMEM)] + [anywhere] * 8,
        out_specs=pl.BlockSpec(memory_space=pltpu.VMEM),
        scratch_shapes=[
            pltpu.VMEM(wide, BF16), pltpu.VMEM(wide, BF16), pltpu.VMEM(wide, BF16),
            pltpu.VMEM(wide, BF16), pltpu.VMEM(kv_wide, BF16), pltpu.VMEM(kv_wide, BF16),
            pltpu.VMEM((heads, HD), BF16), pltpu.VMEM((heads, HD), BF16),
            pltpu.VMEM((2, 2) + kv_wide, BF16),
            pltpu.VMEM(state, F32), pltpu.VMEM((heads, HD, HD), F32),
            pltpu.VMEM(wide, BF16), pltpu.VMEM(wide, F32), pltpu.VMEM(wide, F32),
            pltpu.VMEM(state, SIDE), pltpu.VMEM(state, SIDE),
            pltpu.VMEM(state, CHAIN), pltpu.VMEM(state, CHAIN),
            pltpu.VMEM(state, BACK), pltpu.VMEM(state, BACK),
            pltpu.VMEM((8, tokens), F32), pltpu.VMEM((nt - 1, 8, tokens), F32),
            dma((8,)), dma((2, kv_heads, 2)), dma((2, kv_heads, 2)),
            dma((half,)), dma((half,)), dma((half,)), dma((half,)), dma((half,)), dma((half,)),
            dma((nt - 1,)), dma((nt - 1,)),
        ],
        compiler_params=pltpu.CompilerParams(
            collective_id=0, has_side_effects=True, vmem_limit_bytes=63 * 2 ** 20
        ),
    )(block_lists, lin_q, lin_k, lin_v, att_q, att_k, att_v, gain_lin, gain_att)


def solution(mesh):
    wide = P("ctx", "tp")
    return jax.shard_map(
        functools.partial(per_device, mesh.shape["ctx"], mesh.shape["tp"]),
        mesh=mesh,
        in_specs=(wide,) * 6 + (P("ctx", None), P("tp"), P("tp")),
        out_specs=wide,
        check_vma=False,
    )
```

```python
import functools
import math

import jax
import jax.numpy as jnp
from jax import lax
from jax.experimental import pallas as pl
from jax.experimental.pallas import tpu as pltpu
from jax.sharding import PartitionSpec as P

HD = 128
BLK = 128
SPAN = 5
EPS = 1e-06
NEG = -1e30
MESH = pl.DeviceIdType.MESH
BF16, F32 = jnp.bfloat16, jnp.float32

SIDE = BF16
CHAIN = BF16
BACK = BF16


def dot(a, b, dims):
    return lax.dot_general(a, b, (dims, ((), ())), preferred_element_type=F32)


def kernel(
    n, nt, lists, lin_q_h, lin_k_h, lin_v_h, att_q_h, att_k_h, att_v_h, gain_lin_h, gain_att_h,
    out, lin_q, lin_k, lin_v, att_q, att_k, att_v, gain_lin, gain_att, kv, total, first, scores, lin_out, att_out,
    xout, xin, zout, zin, bout, bin_, sq_out, sq_in,
    lsem, kvs, kvr, xs, xr, zs, zr, bs, br, ns, nr,
):
    ctx, tp = lax.axis_index("ctx"), lax.axis_index("tp")
    p, o = lax.rem(ctx, 2), lax.div(ctx, 2)
    mate = ctx + 1 - 2 * p
    tokens = lin_q.shape[0]
    heads = lin_q.shape[1] // HD
    kv_heads = att_k.shape[1] // HD
    half = heads // 2
    has_prev, has_next = o > 0, o < n // 2 - 1
    side, ahead, behind = {"ctx": mate}, {"ctx": ctx + 2}, {"ctx": ctx - 2}

    pairs = (
        (lin_k_h, lin_k), (lin_v_h, lin_v), (lin_q_h, lin_q),
        (att_q_h, att_q), (att_k_h, att_k), (att_v_h, att_v),
        (gain_lin_h, gain_lin), (gain_att_h, gain_att),
    )
    local = [pltpu.make_async_copy(s, d, lsem.at[i]) for i, (s, d) in enumerate(pairs)]
    for c in local:
        c.start()

    barrier = pltpu.get_barrier_semaphore()

    def greet(where):
        pl.semaphore_signal(barrier, inc=1, device_id=where, device_id_type=MESH)

    greet(side)
    for k in range(1, nt):
        greet({"tp": lax.rem(tp + k, nt)})
    pl.when(has_prev)(lambda: greet(behind))
    pl.when(has_next)(lambda: greet(ahead))
    pl.semaphore_wait(barrier, nt + has_prev.astype(jnp.int32) + has_next.astype(jnp.int32))

    def remote(src, dst, ssem, rsem, where):
        return pltpu.make_async_remote_copy(
            src_ref=src, dst_ref=dst, send_sem=ssem, recv_sem=rsem,
            device_id=where, device_id_type=MESH,
        )

    def kv_copies(src, slot, sem, where):
        return [
            [
                remote(
                    src[a].at[:, pl.ds(g * HD, HD)], kv.at[slot, a, :, pl.ds(g * HD, HD)],
                    kvs.at[sem, g, a], kvr.at[sem, g, a], where,
                )
                for a in range(2)
            ]
            for g in range(kv_heads)
        ]

    kv_src = (att_k_h, att_v_h)
    kv_ahead = kv_copies(kv_src, 1, 1, ahead)
    kv_side = kv_copies(kv_src, 0, 0, side)
    kv_pass = kv_copies((kv.at[1, 0], kv.at[1, 1]), 0, 0, side)

    def send_kv(g):
        for a in range(2):
            pl.when(has_next)(kv_ahead[g][a].start)
            pl.when(p == 0)(kv_side[g][a].start)

    def sent_kv(g):
        for a in range(2):
            pl.when(has_next)(kv_ahead[g][a].wait_send)
            pl.when(p == 0)(kv_side[g][a].wait_send)

    send_kv(0)

    @pl.when(jnp.logical_not(has_prev))
    def _():
        kv[1] = jnp.zeros_like(kv[1])

        @pl.when(p == 0)
        def _():
            kv[0] = jnp.zeros_like(kv[0])

    local[0].wait()
    local[1].wait()

    def lanes(h):
        return pl.ds(pl.multiple_of(h * HD, HD), HD)

    x_copy = [remote(xout.at[j], xin.at[j], xs.at[j], xr.at[j], side) for j in range(half)]
    z_copy = [remote(zout.at[j], zin.at[j], zs.at[j], zr.at[j], ahead) for j in range(half)]
    b_copy = [remote(bout.at[j], bin_.at[j], bs.at[j], br.at[j], side) for j in range(half)]
    other, mine = (1 - p) * half, p * half

    for j in range(half):
        h = other + j
        xout[j] = dot(lin_k[:, lanes(h)], lin_v[:, lanes(h)], ((0,), (0,))).astype(SIDE)
        x_copy[j].start()
    for g in range(1, kv_heads):
        sent_kv(g - 1)
        send_kv(g)
    for j in range(half):
        h = mine + j
        total[j] = dot(lin_k[:, lanes(h)], lin_v[:, lanes(h)], ((0,), (0,)))

    local[2].wait()
    row = lax.broadcasted_iota(jnp.int32, (BLK, BLK), 0)
    col = lax.broadcasted_iota(jnp.int32, (BLK, BLK), 1)
    lower = row >= col
    blocks = tokens // BLK
    for h in range(heads):
        hs = pl.ds(h * HD, HD)
        for b in range(blocks):
            rows = pl.ds(b * BLK, BLK)
            s = dot(lin_q[rows, hs], lin_k[rows, hs], ((1,), (1,)))
            scores[rows, hs] = jnp.where(lower, s, 0.0).astype(BF16)
        first[h] = dot(lin_k[0:BLK, hs], lin_v[0:BLK, hs], ((0,), (0,)))

    def forward(g):
        @pl.when(has_prev)
        def _():
            for a in range(2):
                kv_ahead[g][a].wait_recv()

                @pl.when(p == 1)
                def _():
                    kv_pass[g][a].start()

    def chain():
        for j in range(half):
            @pl.when(has_prev)
            def _():
                z_copy[j].wait_recv()

            @pl.when(jnp.logical_not(has_prev))
            def _():
                zin[j] = jnp.zeros_like(zin[j])

            x_copy[j].wait_recv()
            before = zin[j].astype(F32)
            here, there = total[j], xin[j].astype(F32)
            zout[j] = (before + here + there).astype(CHAIN)
            pl.when(has_next)(z_copy[j].start)
            bout[j] = jnp.where(p == 0, before + here, before).astype(BACK)
            b_copy[j].start()
            total[j] = jnp.where(p == 0, before, before + there)

    for g in range(kv_heads):
        forward(g)
    early = has_next & (o < 2)
    middle = has_next & (o >= 2)
    late = jnp.logical_not(has_next)
    pl.when(early)(chain)
    for c in local[3:]:
        c.wait()
    factor = (HD ** -0.5) * math.log2(math.e)
    cut = (SPAN - 1) * BLK
    bias = []
    for b in range(blocks):
        parts = []
        for i in range(SPAN - 1):
            key_block = ctx * blocks + b - (SPAN - 1) + i
            hit = lists[b, 0] == key_block
            for e in range(1, 4):
                hit = hit | (lists[b, e] == key_block)
            value = jnp.where(hit & (key_block >= 0), 0.0, NEG).astype(F32)
            parts.append(jnp.full((1, BLK), value, F32))
        bias.append(jnp.concatenate(parts, axis=1))

    att_sq = [None] * blocks

    def attend(g):
        gs = pl.ds(g * HD, HD)
        for a in range(2):
            @pl.when((p == 1) | has_prev)
            def _():
                kv_side[g][a].wait_recv()

        for b in range(blocks):
            rows = pl.ds(b * BLK, BLK)

            def window(a, own):
                parts = [kv[1, a, b * BLK:, gs], kv[0, a, :, gs], own[: (b + 1) * BLK, gs]]
                return jnp.concatenate(parts, axis=0)

            keys, values = window(0, att_k), window(1, att_v)
            group = range(g * heads // kv_heads, (g + 1) * heads // kv_heads)
            queries = jnp.concatenate([att_q[rows, pl.ds(h * HD, HD)] for h in group], axis=0)
            sall = dot(queries, keys, ((1,), (1,)))
            wall = []
            for i in range(len(group)):
                s = sall[i * BLK:(i + 1) * BLK]
                s = jnp.concatenate(
                    [s[:, :cut] + bias[b], jnp.where(lower, s[:, cut:], NEG)], axis=1
                )
                e = jnp.exp2((s - jnp.max(s, axis=1, keepdims=True)) * factor)
                wall.append((e * (1.0 / jnp.sum(e, axis=1, keepdims=True))).astype(BF16))
            rall = dot(jnp.concatenate(wall, axis=0), values, ((1,), (0,)))
            for i, h in enumerate(group):
                r = rall[i * BLK:(i + 1) * BLK]
                att_out[rows, pl.ds(h * HD, HD)] = r
                att_sq[b] = r * r if att_sq[b] is None else att_sq[b] + r * r

    for g in range(kv_heads):
        attend(g)
        if g == 0:
            pl.when(middle)(chain)
    pl.when(late)(chain)
    lin_sq = [None] * blocks

    def finish(h, prefix):
        for b in range(blocks):
            rows = pl.ds(b * BLK, BLK)
            low = (prefix if b == 0 else prefix + first[h]).astype(BF16)
            lhs = jnp.concatenate([scores[rows, lanes(h)], lin_q[rows, lanes(h)]], axis=1)
            rhs = jnp.concatenate([lin_v[rows, lanes(h)], low], axis=0)
            r = dot(lhs, rhs, ((1,), (0,)))
            lin_out[rows, lanes(h)] = r
            lin_sq[b] = r * r if lin_sq[b] is None else lin_sq[b] + r * r

    for j in range(half):
        finish(mine + j, total[j])
    for j in range(half):
        b_copy[j].wait_recv()
        finish(other + j, bin_[j].astype(F32))

    def as_row(parts):
        return jnp.sum(jnp.concatenate(parts, axis=0).T, axis=0, keepdims=True)

    top = lax.broadcasted_iota(jnp.int32, (8, tokens), 0) == 0
    sums = jnp.where(top, as_row(lin_sq), as_row(att_sq))
    sq_out[...] = sums
    n_copy = [
        remote(sq_out, sq_in.at[k - 1], ns.at[k - 1], nr.at[k - 1], {"tp": lax.rem(tp + k, nt)})
        for k in range(1, nt)
    ]
    for c in n_copy:
        c.start()
    sent_kv(kv_heads - 1)
    @pl.when((p == 1) & has_prev)
    def _():
        for g in range(kv_heads):
            for a in range(2):
                kv_pass[g][a].wait_send()
    for j in range(half):
        x_copy[j].wait_send()
        pl.when(has_next)(z_copy[j].wait_send)
        b_copy[j].wait_send()
    for k in range(nt - 1):
        n_copy[k].wait_recv()
        sums = sums + sq_in[k]
    inv = lax.rsqrt(sums * (1.0 / (nt * heads * HD)) + EPS)

    def as_column(r):
        return jnp.broadcast_to(r, (HD, tokens)).T

    lin_inv, att_inv = as_column(inv[0:1]), as_column(inv[1:2])
    gl, ga = gain_lin[...].astype(F32), gain_att[...].astype(F32)
    for h in range(heads):
        hs = pl.ds(h * HD, HD)
        out[:, hs] = (
            lin_out[:, hs] * lin_inv * gl[h:h + 1] + att_out[:, hs] * att_inv * ga[h:h + 1]
        ).astype(BF16)
    for c in n_copy:
        c.wait_send()


def per_device(n, nt, lin_q, lin_k, lin_v, att_q, att_k, att_v, block_lists, gain_lin, gain_att):
    tokens, columns = lin_q.shape
    heads, half = columns // HD, columns // HD // 2
    gain_lin, gain_att = gain_lin.reshape(heads, HD), gain_att.reshape(heads, HD)
    anywhere = pl.BlockSpec(memory_space=pl.ANY)
    wide, kv_wide = (tokens, columns), att_k.shape
    state, kv_heads = (half, HD, HD), kv_wide[1] // HD
    dma = pltpu.SemaphoreType.DMA
    return pl.pallas_call(
        functools.partial(kernel, n, nt),
        out_shape=pltpu.VMEM(wide, BF16),
        in_specs=[pl.BlockSpec(memory_space=pltpu.SMEM)] + [anywhere] * 8,
        out_specs=pl.BlockSpec(memory_space=pltpu.VMEM),
        scratch_shapes=[
            pltpu.VMEM(wide, BF16), pltpu.VMEM(wide, BF16), pltpu.VMEM(wide, BF16),
            pltpu.VMEM(wide, BF16), pltpu.VMEM(kv_wide, BF16), pltpu.VMEM(kv_wide, BF16),
            pltpu.VMEM((heads, HD), BF16), pltpu.VMEM((heads, HD), BF16),
            pltpu.VMEM((2, 2) + kv_wide, BF16),
            pltpu.VMEM(state, F32), pltpu.VMEM((heads, HD, HD), F32),
            pltpu.VMEM(wide, BF16), pltpu.VMEM(wide, F32), pltpu.VMEM(wide, F32),
            pltpu.VMEM(state, SIDE), pltpu.VMEM(state, SIDE),
            pltpu.VMEM(state, CHAIN), pltpu.VMEM(state, CHAIN),
            pltpu.VMEM(state, BACK), pltpu.VMEM(state, BACK),
            pltpu.VMEM((8, tokens), F32), pltpu.VMEM((nt - 1, 8, tokens), F32),
            dma((8,)), dma((2, kv_heads, 2)), dma((2, kv_heads, 2)),
            dma((half,)), dma((half,)), dma((half,)), dma((half,)), dma((half,)), dma((half,)),
            dma((nt - 1,)), dma((nt - 1,)),
        ],
        compiler_params=pltpu.CompilerParams(
            collective_id=0, has_side_effects=True, vmem_limit_bytes=63 * 2 ** 20
        ),
    )(block_lists, lin_q, lin_k, lin_v, att_q, att_k, att_v, gain_lin, gain_att)


def solution(mesh):
    wide = P("ctx", "tp")
    return jax.shard_map(
        functools.partial(per_device, mesh.shape["ctx"], mesh.shape["tp"]),
        mesh=mesh,
        in_specs=(wide,) * 6 + (P("ctx", None), P("tp"), P("tp")),
        out_specs=wide,
        check_vma=False,
    )
```
